256 devices in a mesh: tok: 32 (over y, z), head: 8 (over x, core).
Axes of the slice: x: 4, y: 4, z: 8, core: 2. Of those that a mesh axis runs over, the one named last changes fastest.
Arguments:
- queries: bfloat16 [16384, 4096], P(('tok', 'head')), may hold values from -6 to 6
- keys: bfloat16 [16384, 4096], P(('tok', 'head')), may hold values from -6 to 6
- values: bfloat16 [16384, 4096], P(('tok', 'head')), may hold values from -6 to 6
- rates: bfloat16 [16384, 16], P(('tok', 'head')), may hold values from 0.03 to 1
- item_ids: int32 [16384], P('tok'), may hold values from 0 to 4095
- boundary: int32 [1], replicated, may hold values from 4096 to 12288
- item_table: bfloat16 [4096, 4096], P(None, 'head'), may hold values from -3 to 3
- w_first: float32 [16, 256, 512], P('head'), may hold values from -0.375 to 0.375
- w_third: float32 [16, 256, 512], P('head'), may hold values from -0.375 to 0.375
- w_out: float32 [16, 256, 512], P('head'), may hold values from -0.25 to 0.25
Outputs:
- layer_output: bfloat16 [16384, 4096], P(('tok', 'head'))
The draws below stay inside these ranges and needn't reach their ends.
Inputs may be any that keep to these rules, and one draw needn't show every extreme that they name: `boundary`: each stretch holds a quarter of the 16384 positions or more.
All inputs are finite; a program needn't handle non-finite values.
Results may differ from the reference program's by a relative error of at most 0.02.
Values may be sent and summed in bfloat16 or wider, within the bound.
A program may use at most 128 MiB of HBM per device.

```python
import math
import jax
import jax.numpy as jnp
import numpy as np
from jax import lax

D = 4096
HEADS = 16
HD = 256
FH = 512
ITEMS = 4096
NS_ITERS = 3
TOKENS = 16384


def draw_rates(key, part):
    position = jnp.arange(TOKENS, dtype=jnp.float32) / TOKENS
    base = 0.1 * (1.0 + 2.0 * position)[:, None]
    rough = jnp.exp(jax.random.uniform(key, (TOKENS, HEADS), jnp.float32, -1.0, 1.0))
    return (base * rough).astype(jnp.bfloat16)


def with_ends(entries, rng, low, top_value):
    place = [jax.random.randint(jax.random.fold_in(rng, axis), (), 0, length) for axis, length in enumerate(entries.shape)]
    main_axis = entries.shape.index(max(entries.shape))
    beside = place[:main_axis] + [(place[main_axis] + 1) % entries.shape[main_axis]] + place[main_axis + 1:]
    return entries.at[tuple(place)].set(low).at[tuple(beside)].set(top_value)


def shard_levels(key, shape, pieces, low, top_value):
    factor_of = 1.0
    for axis_at, blocks in pieces:
        draws = jax.random.uniform(jax.random.fold_in(jax.random.fold_in(key, 6), axis_at), (blocks,), jnp.float32, low / len(pieces), top_value / len(pieces))
        factor_of = factor_of * jnp.repeat(jnp.exp(draws), shape[axis_at] // blocks).reshape((-1,) + (1,) * (len(shape) - 1 - axis_at))
    return factor_of


def rank_bounds(amount, skew):
    weights = [(1 << 20) // math.isqrt(grade ** skew) + 1 for grade in range(1, amount + 1)]
    deviation = 1 + sum(weights) // (1 << 30)
    return np.cumsum(np.array([max(1, weight // deviation) for weight in weights]))


def skewed_ids(own_key, shape, amount, lean):
    grid = rank_bounds(amount, lean)
    ticket = jax.random.randint(jax.random.fold_in(own_key, 1), shape, 0, int(grid[amount - 1]))
    standing = jnp.searchsorted(jnp.asarray(grid, jnp.int32), ticket, side="right")
    return jax.random.permutation(jax.random.fold_in(own_key, 2), amount)[standing].astype(jnp.int32)


def bell_draw(own_key, shape, spread, reach, shards=(), held_as=jnp.bfloat16):
    gain = shard_levels(own_key, shape, shards, -0.22, 0.18) if shards else 1.0
    entries = jax.random.normal(own_key, shape, jnp.float32) * spread * gain
    return jnp.minimum(jnp.maximum(entries, -reach), reach).astype(held_as)


def setup_inputs(seed: int = 0) -> dict:
    seeds = jax.random.split(jax.random.key(seed), 11)
    return {
        "queries": bell_draw(seeds[0], (TOKENS, D), 1.0, 6.0, ((0, 256),)),
        "keys": bell_draw(seeds[1], (TOKENS, D), 1.0, 6.0, ((0, 256),)),
        "values": bell_draw(seeds[2], (TOKENS, D), 1.0, 6.0, ((0, 256),)),
        "rates": draw_rates(jax.random.fold_in(seeds[10], 71), 0),
        "item_ids": with_ends(skewed_ids(seeds[4], (TOKENS,), ITEMS, 2), jax.random.fold_in(seeds[4], 3), 0, ITEMS - 1).astype(jnp.int32),
        "boundary": jax.random.randint(seeds[5], (1,), TOKENS // 4, 3 * TOKENS // 4 + 1).astype(jnp.int32),
        "item_table": bell_draw(seeds[6], (ITEMS, D), 0.5, 3.0, ((1, 8),)),
        "w_first": bell_draw(seeds[7], (HEADS, HD, FH), HD ** -0.5, 0.375, ((0, 8),), jnp.float32),
        "w_third": bell_draw(seeds[8], (HEADS, HD, FH), HD ** -0.5, 0.375, ((0, 8),), jnp.float32),
        "w_out": bell_draw(seeds[9], (HEADS, HD, FH), FH ** -0.5, 0.25, ((0, 8),), jnp.float32),
    }


highest = lax.Precision.HIGHEST
coeff_first = 3.4445
coeff_second = -4.775
coeff_third = 2.0315

def orthogonal(gradient):
    scaled = gradient / (jnp.sqrt(jnp.sum(gradient * gradient)) + 1e-06)
    for repeat in range(NS_ITERS):
        gram_matrix = jnp.dot(scaled, scaled.T, precision=highest)
        polynomial = coeff_second * gram_matrix + coeff_third * jnp.dot(gram_matrix, gram_matrix, precision=highest)
        scaled = coeff_first * scaled + jnp.dot(polynomial, scaled, precision=highest)
    return scaled

def reference(queries, keys, values, rates, item_ids, boundary, item_table, w_first, w_third, w_out):
    split_at = boundary[0]
    target = values.astype(jnp.float32) + jnp.take(item_table, item_ids, axis=0).astype(jnp.float32)

    def by_head(array):
        return jnp.transpose(array.reshape(TOKENS, HEADS, HD), (1, 0, 2))
    positions = jnp.arange(TOKENS, dtype=jnp.int32)
    members = [positions < split_at, positions >= split_at]
    counts = [split_at.astype(jnp.float32), (TOKENS - split_at).astype(jnp.float32)]

    def one_head(inputs):
        key_rows, target_rows, query_rows, rate_rows, first, third, output_w = inputs
        result = jnp.zeros((TOKENS, HD), jnp.float32)
        for segment in range(2):
            member = members[segment].astype(jnp.float32)
            weighted = member * rate_rows
            step_size = jnp.sum(weighted) / counts[segment]
            first_low = first.astype(jnp.bfloat16)
            third_low = third.astype(jnp.bfloat16)
            output_low = output_w.astype(jnp.bfloat16)
            first_pre = jnp.dot(key_rows, first_low, preferred_element_type=jnp.float32)
            third_pre = jnp.dot(key_rows, third_low, preferred_element_type=jnp.float32)
            activation = (jax.nn.silu(first_pre) * third_pre).astype(jnp.bfloat16)
            upstream = (-weighted[:, None] * target_rows).astype(jnp.bfloat16)
            grad_out = jnp.dot(upstream.T, activation, preferred_element_type=jnp.float32)
            back_activ = jnp.dot(upstream, output_low, preferred_element_type=jnp.float32)
            sigmoid_pre = jax.nn.sigmoid(first_pre)
            silu_slope = sigmoid_pre * (1.0 + first_pre * (1.0 - sigmoid_pre))
            back_first = (back_activ * third_pre * silu_slope).astype(jnp.bfloat16)
            back_third = (back_activ * jax.nn.silu(first_pre)).astype(jnp.bfloat16)
            grad_first = jnp.dot(key_rows.T, back_first, preferred_element_type=jnp.float32)
            grad_third = jnp.dot(key_rows.T, back_third, preferred_element_type=jnp.float32)
            first = first - step_size * orthogonal(grad_first)
            third = third - step_size * orthogonal(grad_third)
            output_w = output_w - step_size * orthogonal(grad_out)
            query_first = jnp.dot(query_rows, first.astype(jnp.bfloat16), preferred_element_type=jnp.float32)
            query_third = jnp.dot(query_rows, third.astype(jnp.bfloat16), preferred_element_type=jnp.float32)
            query_act = (jax.nn.silu(query_first) * query_third).astype(jnp.bfloat16)
            applied = jnp.dot(query_act, output_w.astype(jnp.bfloat16).T, preferred_element_type=jnp.float32)
            result = jnp.where(members[segment][:, None], applied, result)
        return result
    outputs = lax.map(one_head, (by_head(keys), by_head(target), by_head(queries), rates.astype(jnp.float32).T, w_first, w_third, w_out))
    return jnp.transpose(outputs, (1, 0, 2)).reshape(TOKENS, D).astype(jnp.bfloat16)
```

```python
import functools

import jax
import jax.numpy as jnp
from jax import lax
from jax.experimental import pallas as pl
from jax.experimental.pallas import tpu as pltpu
from jax.sharding import PartitionSpec as P

MESH = pl.DeviceIdType.MESH
F32, BF16 = jnp.float32, jnp.bfloat16

NY, NZ = 4, 8
NQ = NZ // 2
NH = 8
ROWS, D, HD, FH, ITEMS, TOKENS = 64, 4096, 256, 512, 4096, 16384
SRC = 2 * NH
LOCAL = SRC * ROWS
YR, ZR = HD // NY, HD // NY // NQ
NS_ITERS = 3
C1, C2, C3 = 3.4445, -4.775, 2.0315
TILE = 256
ITEM_TILE = 512


def dot(a, b):
    return jnp.dot(a, b, preferred_element_type=F32)


def dot_rows(a, b):
    return lax.dot_general(a, b, (((0,), (0,)), ((), ())), preferred_element_type=F32)


def dot_cols(a, b):
    return lax.dot_general(a, b, (((1,), (1,)), ((), ())), preferred_element_type=F32)


def sigmoid(u):
    return 0.5 * jnp.tanh(0.5 * u) + 0.5


def kernel(
    q_ref, k_ref, v_ref, rate_ref, ids_ref, bound_ref, table_ref, w1_ref, w3_ref, w2_ref,
    out_ref,
    kb, vb, qb, rb_in, ids_in, table, w, wl, rates, idcol, looked, g, gl,
    ybuf, zown, zsend, zbuf, final, rsum, rsum_y, rsum_z, result, outb,
    tok_send, tok_recv, id_send, id_recv, y_send, y_recv, z_send, z_recv,
    az_send, az_recv, ay_send, ay_recv, ry_send, ry_recv, rz_send, rz_recv,
    out_send, out_recv, local_sem,
):
    t, h = lax.axis_index("tok"), lax.axis_index("head")
    y, z = lax.div(t, NZ), lax.rem(t, NZ)
    p, zq = lax.rem(z, 2), lax.div(z, 2)
    me = p * NH + h
    pair = t - p

    def remote(src, dst, send, recv, tok, head):
        return pltpu.make_async_remote_copy(
            src_ref=src, dst_ref=dst, send_sem=send, recv_sem=recv,
            device_id={"tok": tok, "head": head}, device_id_type=MESH,
        )

    def source(n):
        s = lax.rem(me + n, SRC)
        return s, pair + lax.div(s, NH), lax.rem(s, NH)

    def y_peer(n):
        i = lax.rem(y + n, NY)
        return i, i * NZ + z

    def z_peer(n):
        i = lax.rem(zq + n, NQ)
        return i, y * NZ + 2 * i + p

    lanes = pl.ds(pl.multiple_of(p * HD, HD), HD)
    copies = [
        pltpu.make_async_copy(table_ref.at[:, lanes], table, local_sem.at[0]),
        pltpu.make_async_copy(w1_ref.at[p], w.at[0], local_sem.at[1]),
        pltpu.make_async_copy(w3_ref.at[p], w.at[1], local_sem.at[2]),
        pltpu.make_async_copy(w2_ref.at[p], w.at[2], local_sem.at[3]),
    ]
    own = pl.ds(pl.multiple_of(me * ROWS, ROWS), ROWS)
    my_cols = pl.ds(pl.multiple_of((2 * h + p) * HD, HD), HD)
    own_copies = [
        pltpu.make_async_copy(k_ref.at[:, my_cols], kb.at[own], local_sem.at[4]),
        pltpu.make_async_copy(v_ref.at[:, my_cols], vb.at[own], local_sem.at[5]),
        pltpu.make_async_copy(q_ref.at[:, my_cols], qb.at[own], local_sem.at[6]),
        pltpu.make_async_copy(rate_ref.at[2 * h + p], rb_in.at[me], local_sem.at[7]),
        pltpu.make_async_copy(ids_ref, ids_in.at[p], local_sem.at[8]),
    ]
    for copy in own_copies + copies:
        copy.start()

    barrier = pltpu.get_barrier_semaphore()
    for n in range(1, SRC):
        _, tok, head = source(n)
        pl.semaphore_signal(barrier, inc=1, device_id={"tok": tok, "head": head}, device_id_type=MESH)
    for n in range(1, NY):
        pl.semaphore_signal(barrier, inc=1, device_id={"tok": y_peer(n)[1], "head": h}, device_id_type=MESH)
    for n in range(1, NQ):
        pl.semaphore_signal(barrier, inc=1, device_id={"tok": z_peer(n)[1], "head": h}, device_id_type=MESH)
    pl.semaphore_wait(barrier, SRC - 1 + NY - 1 + NQ - 1)

    id_copy = remote(ids_ref, ids_in.at[p], id_send, id_recv, pair + 1 - p, h)
    id_copy.start()

    def token_copies(kind):
        src, dst = ((k_ref, kb), (v_ref, vb), (q_ref, qb), (rate_ref, rb_in))[kind]
        made = []
        for n in range(1, SRC):
            s, tok, head = source(n)
            head_no = 2 * head + lax.div(s, NH)
            if kind == 3:
                a, b = src.at[head_no], dst.at[me]
            else:
                a = src.at[:, pl.ds(pl.multiple_of(head_no * HD, HD), HD)]
                b = dst.at[own]
            made.append(remote(a, b, tok_send.at[kind, s], tok_recv.at[kind, me], tok, head))
        return made

    def token_wait(kind):
        dst = (kb, vb, qb, rb_in)[kind]
        for n in range(1, SRC):
            s, tok, head = source(n)
            b = dst.at[s] if kind == 3 else dst.at[pl.ds(pl.multiple_of(s * ROWS, ROWS), ROWS)]
            remote(b, b, tok_send.at[kind, s], tok_recv.at[kind, s], tok, head).wait_recv()

    rate_copies = token_copies(3)
    key_copies = token_copies(0)
    value_copies = token_copies(1)
    query_copies = token_copies(2)
    for copy in rate_copies + key_copies + value_copies:
        copy.start()

    id_copy.wait_send()
    other_ids = ids_in.at[1 - p]
    remote(other_ids, other_ids, id_send, id_recv, pair + 1 - p, h).wait_recv()
    for copy in own_copies + copies:
        copy.wait()
    eye = lax.broadcasted_iota(jnp.int32, (128, 128), 0) == lax.broadcasted_iota(jnp.int32, (128, 128), 1)
    for half in range(2):
        for group in range(4):
            row = ids_in[half, group : group + 1, :]
            column = jnp.sum(jnp.where(eye, row, 0.0), axis=1, keepdims=True)
            idcol[pl.ds(half * 512 + group * 128, 128), :] = jnp.broadcast_to(column, (128, 128))

    lane = lax.broadcasted_iota(jnp.int32, (TILE, 128), 1).astype(F32)

    def look(i, _):
        rows = pl.ds(pl.multiple_of(i * TILE, TILE), TILE)
        ids = idcol[rows, :]

        def part(j, total):
            first = (j * ITEM_TILE).astype(F32)
            hot = jnp.concatenate(
                [jnp.where(ids - first == lane + 128.0 * b, 1.0, 0.0).astype(BF16) for b in range(ITEM_TILE // 128)],
                axis=1,
            )
            items = pl.ds(pl.multiple_of(j * ITEM_TILE, ITEM_TILE), ITEM_TILE)
            return total + dot(hot, table[items, :])

        looked[rows, :] = lax.fori_loop(0, ITEMS // ITEM_TILE, part, jnp.zeros((TILE, HD), F32)).astype(BF16)
        return 0

    lax.fori_loop(0, LOCAL // TILE, look, 0)

    token_wait(3)
    for s in range(SRC):
        row = rb_in[s]
        column = jnp.sum(jnp.where(eye[:ROWS], row, 0.0), axis=1, keepdims=True)
        rates[pl.ds(s * ROWS, ROWS), :] = jnp.broadcast_to(column, (ROWS, 128))

    split_at = bound_ref[0]
    first_row = pair * (TOKENS // (NY * NZ))

    def member(segment, start, size, width):
        positions = first_row + start + lax.broadcasted_iota(jnp.int32, (size, width), 0)
        return positions < split_at if segment == 0 else positions >= split_at

    sums = [
        jnp.sum(jnp.where(member(c, 0, LOCAL, 128), rates[...], 0.0), axis=0, keepdims=True) for c in range(2)
    ]
    rsum[...] = jnp.concatenate([jnp.broadcast_to(v, (8, 128)) for v in sums], axis=0)
    rate_y = []
    for n in range(1, NY):
        i, tok = y_peer(n)
        rate_y.append(remote(rsum, rsum_y.at[y], ry_send.at[i], ry_recv.at[y], tok, h))
        rate_y[-1].start()
    for n in range(1, NY):
        i, tok = y_peer(n)
        remote(rsum, rsum_y.at[i], ry_send.at[i], ry_recv.at[i], tok, h).wait_recv()
        sums_y = rsum[...] if n == 1 else sums_y
        sums_y = sums_y + rsum_y[i]
    rsum_z[zq] = sums_y
    rate_z = []
    for n in range(1, NQ):
        i, tok = z_peer(n)
        rate_z.append(remote(rsum_z.at[zq], rsum_z.at[zq], rz_send.at[i], rz_recv.at[zq], tok, h))
        rate_z[-1].start()

    token_wait(0)
    token_wait(1)
    for copy in query_copies:
        copy.start()

    def queries(segment):
        def body(i, _):
            rows = pl.ds(pl.multiple_of(i * TILE, TILE), TILE)
            x = qb[rows, :]
            first_pre, third_pre = dot(x, wl[0]), dot(x, wl[1])
            act = (first_pre * sigmoid(first_pre) * third_pre).astype(BF16)
            applied = dot_cols(act, wl[2])
            if segment == 0:
                result[rows, :] = applied
            else:
                keep = member(1, i * TILE, TILE, HD)
                outb[rows, :] = jnp.where(keep, applied, result[rows, :]).astype(BF16)
            return 0

        lax.fori_loop(0, LOCAL // TILE, body, 0)

    def low(m):
        wl[m] = w[m].astype(BF16)

    for m in range(3):
        low(m)

    waiting = []
    for c in range(2):

        def gradient(i, _, c=c):
            rows = pl.ds(pl.multiple_of(i * TILE, TILE), TILE)
            key = kb[rows, :]
            keep = member(c, i * TILE, TILE, 128)
            weighted = jnp.where(keep, rates[rows, :], 0.0)
            weighted = jnp.concatenate([weighted, weighted], axis=1)
            target = vb[rows, :].astype(F32) + looked[rows, :].astype(F32)
            upstream = (-weighted * target).astype(BF16)
            first_pre, third_pre = dot(key, wl[0]), dot(key, wl[1])
            back = dot(upstream, wl[2])
            s = sigmoid(first_pre)
            silu = first_pre * s
            act = (silu * third_pre).astype(BF16)
            back1 = (back * third_pre * (s * (1.0 + first_pre * (1.0 - s)))).astype(BF16)
            back3 = (back * silu).astype(BF16)
            parts = (dot_rows(key, back1), dot_rows(key, back3), dot_rows(upstream, act))
            for m in range(3):
                g[m] = parts[m] + jnp.where(i == 0, 0.0, g[m])
            return 0

        lax.fori_loop(0, LOCAL // TILE, gradient, 0)

        for m in range(3):
            gl[c, m] = g[m].astype(BF16)
            for n in range(1, NY):
                i, tok = y_peer(n)
                block = gl.at[c, m, pl.ds(pl.multiple_of(i * YR, YR), YR)]
                copy = remote(block, ybuf.at[c, m, y], y_send.at[c, m, i], y_recv.at[c, m, y], tok, h)
                copy.start()
                waiting.append(copy)

        if c == 1:
            token_wait_done = queries(0)
        my_y = pl.ds(pl.multiple_of(y * YR, YR), YR)
        my_z = pl.ds(pl.multiple_of(zq * ZR, ZR), ZR)
        mine = pl.ds(pl.multiple_of(y * YR + zq * ZR, ZR), ZR)
        for m in range(3):
            total = g[m, my_y, :]
            for n in range(1, NY):
                i, tok = y_peer(n)
                remote(ybuf.at[c, m, i], ybuf.at[c, m, i], y_send.at[c, m, i], y_recv.at[c, m, i], tok, h).wait_recv()
                total = total + ybuf[c, m, i].astype(F32)
            zown[m] = total
            zsend[c, m] = total.astype(BF16)
            for n in range(1, NQ):
                i, tok = z_peer(n)
                block = zsend.at[c, m, pl.ds(pl.multiple_of(i * ZR, ZR), ZR)]
                copy = remote(block, zbuf.at[c, m, zq], z_send.at[c, m, i], z_recv.at[c, m, zq], tok, h)
                copy.start()
                waiting.append(copy)
        for m in range(3):
            total = zown[m, my_z, :]
            for n in range(1, NQ):
                i, tok = z_peer(n)
                remote(zbuf.at[c, m, i], zbuf.at[c, m, i], z_send.at[c, m, i], z_recv.at[c, m, i], tok, h).wait_recv()
                total = total + zbuf[c, m, i].astype(F32)
            final[c, m, mine, :] = total.astype(BF16)
            for n in range(1, NQ):
                i, tok = z_peer(n)
                block = final.at[c, m, mine]
                copy = remote(block, block, az_send.at[c, m, i], az_recv.at[c, m, zq], tok, h)
                copy.start()
                waiting.append(copy)
        for m in range(3):
            for n in range(1, NQ):
                i, tok = z_peer(n)
                block = final.at[c, m, pl.ds(pl.multiple_of(y * YR + i * ZR, ZR), ZR)]
                remote(block, block, az_send.at[c, m, i], az_recv.at[c, m, i], tok, h).wait_recv()
            for n in range(1, NY):
                i, tok = y_peer(n)
                block = final.at[c, m, my_y]
                copy = remote(block, block, ay_send.at[c, m, i], ay_recv.at[c, m, y], tok, h)
                copy.start()
                waiting.append(copy)
        if c == 0:
            for n in range(1, NQ):
                i, tok = z_peer(n)
                remote(rsum_z.at[i], rsum_z.at[i], rz_send.at[i], rz_recv.at[i], tok, h).wait_recv()
            for copy in rate_y + rate_z:
                copy.wait_send()
            sums_all = rsum_z[0] + rsum_z[1] + rsum_z[2] + rsum_z[3]
            counts = [split_at.astype(F32), (TOKENS - split_at).astype(F32)]
            rsum[...] = sums_all
        step = rsum[8 * c : 8 * c + 1, 0:1] / counts[c]
        for m in range(3):
            for n in range(1, NY):
                i, tok = y_peer(n)
                block = final.at[c, m, pl.ds(pl.multiple_of(i * YR, YR), YR)]
                remote(block, block, ay_send.at[c, m, i], ay_recv.at[c, m, i], tok, h).wait_recv()
            x = final[c, m].astype(F32)
            x = x / (jnp.sqrt(jnp.sum(x * x, keepdims=True)) + 1e-06)
            for _ in range(NS_ITERS):
                xl = x.astype(BF16)
                gram = dot_cols(xl, xl)
                gram_low = gram.astype(BF16)
                poly = C2 * gram + C3 * dot(gram_low, gram_low)
                x = C1 * x + dot(poly.astype(BF16), xl)
            w[m] = w[m] - step * x
            low(m)
        if c == 0:
            token_wait(2)
    queries(1)

    sends = []
    for n in range(1, SRC):
        s, tok, head = source(n)
        block = outb.at[pl.ds(pl.multiple_of(s * ROWS, ROWS), ROWS)]
        sends.append(remote(block, out_ref.at[:, my_cols], out_send.at[s], out_recv.at[me], tok, head))
        sends[-1].start()
    mine_copy = pltpu.make_async_copy(outb.at[own], out_ref.at[:, my_cols], local_sem.at[9])
    mine_copy.start()
    for copy in rate_copies + key_copies + value_copies + query_copies + waiting + sends:
        copy.wait_send()
    for n in range(1, SRC):
        s, tok, head = source(n)
        block = out_ref.at[:, pl.ds(pl.multiple_of((2 * head + lax.div(s, NH)) * HD, HD), HD)]
        remote(block, block, out_send.at[s], out_recv.at[s], tok, head).wait_recv()
    mine_copy.wait()


def shards(queries, keys, values, rates, item_ids, boundary, item_table, w_first, w_third, w_out):
    by_head = jnp.pad(rates.T.astype(F32), ((0, 0), (0, 128 - ROWS)))[:, None, :]
    ids = jnp.pad(item_ids.astype(F32).reshape(4, 128), ((0, 4), (0, 0)))
    hbm = pl.BlockSpec(memory_space=pl.ANY)
    vmem = pl.BlockSpec(memory_space=pltpu.VMEM)
    dma = pltpu.SemaphoreType.DMA
    return pl.pallas_call(
        kernel,
        out_shape=jax.ShapeDtypeStruct((ROWS, D), BF16),
        in_specs=[hbm, hbm, hbm, vmem, vmem, pl.BlockSpec(memory_space=pltpu.SMEM), hbm, hbm, hbm, hbm],
        out_specs=hbm,
        scratch_shapes=[
            pltpu.VMEM((LOCAL, HD), BF16),
            pltpu.VMEM((LOCAL, HD), BF16),
            pltpu.VMEM((LOCAL, HD), BF16),
            pltpu.VMEM((SRC, 1, 128), F32),
            pltpu.VMEM((2, 8, 128), F32),
            pltpu.VMEM((ITEMS, HD), BF16),
            pltpu.VMEM((3, HD, FH), F32),
            pltpu.VMEM((3, HD, FH), BF16),
            pltpu.VMEM((LOCAL, 128), F32),
            pltpu.VMEM((LOCAL, 128), F32),
            pltpu.VMEM((LOCAL, HD), BF16),
            pltpu.VMEM((3, HD, FH), F32),
            pltpu.VMEM((2, 3, HD, FH), BF16),
            pltpu.VMEM((2, 3, NY, YR, FH), BF16),
            pltpu.VMEM((3, YR, FH), F32),
            pltpu.VMEM((2, 3, YR, FH), BF16),
            pltpu.VMEM((2, 3, NQ, ZR, FH), BF16),
            pltpu.VMEM((2, 3, HD, FH), BF16),
            pltpu.VMEM((16, 128), F32),
            pltpu.VMEM((NY, 16, 128), F32),
            pltpu.VMEM((NQ, 16, 128), F32),
            pltpu.VMEM((LOCAL, HD), F32),
            pltpu.VMEM((LOCAL, HD), BF16),
            dma((4, SRC)), dma((4, SRC)), dma, dma,
            dma((2, 3, NY)), dma((2, 3, NY)), dma((2, 3, NQ)), dma((2, 3, NQ)),
            dma((2, 3, NQ)), dma((2, 3, NQ)), dma((2, 3, NY)), dma((2, 3, NY)),
            dma((NY,)), dma((NY,)), dma((NQ,)), dma((NQ,)),
            dma((SRC,)), dma((SRC,)), dma((10,)),
        ],
        compiler_params=pltpu.CompilerParams(
            collective_id=0, has_side_effects=True, vmem_limit_bytes=60 * 1024 * 1024
        ),
        name="layer",
    )(queries, keys, values, by_head, ids, boundary, item_table, w_first, w_third, w_out)


def solution(mesh):
    in_specs = (
        P(("tok", "head"), None),
        P(("tok", "head"), None),
        P(("tok", "head"), None),
        P(("tok", "head"), None),
        P("tok"),
        P(),
        P(None, "head"),
        P("head", None, None),
        P("head", None, None),
        P("head", None, None),
    )
    out_specs = P(("tok", "head"), None)
    return jax.shard_map(shards, mesh=mesh, in_specs=in_specs, out_specs=out_specs, check_vma=False)
```

```python
import functools

import jax
import jax.numpy as jnp
from jax import lax
from jax.experimental import pallas as pl
from jax.experimental.pallas import tpu as pltpu
from jax.sharding import PartitionSpec as P

MESH = pl.DeviceIdType.MESH
F32, BF16 = jnp.float32, jnp.bfloat16

NY, NZ = 4, 8
NQ = NZ // 2
NH = 8
ROWS, D, HD, FH, ITEMS, TOKENS = 64, 4096, 256, 512, 4096, 16384
SRC = 2 * NH
LOCAL = SRC * ROWS
YR, ZR = HD // NY, HD // NY // NQ
NS_ITERS = 3
C1, C2, C3 = 3.4445, -4.775, 2.0315
TILE = 256
FT = FH // 2
FT = FH // 2
FT = FH // 2
FT = FH // 2
FT = FH // 2
FT = FH // 2
ITEM_TILE = 512


def dot(a, b):
    return jnp.dot(a, b, preferred_element_type=F32)


def dot_rows(a, b):
    return lax.dot_general(a, b, (((0,), (0,)), ((), ())), preferred_element_type=F32)


def dot_cols(a, b):
    return lax.dot_general(a, b, (((1,), (1,)), ((), ())), preferred_element_type=F32)


def sigmoid(u):
    return 0.5 * jnp.tanh(0.5 * u) + 0.5


def kernel(
    q_ref, k_ref, v_ref, rate_ref, ids_ref, bound_ref, table_ref, w1_ref, w3_ref, w2_ref,
    out_ref,
    kb, vb, qb, rate_all, rate_rows, rb_in, ids_in, table, w, wl, rates, idcol, looked, up, acts, gate, slope, g, gl,
    ybuf, zown, zsend, zbuf, final, rsum, rsum_y, rsum_z, result, outb,
    tok_send, tok_recv, id_send, id_recv, y_send, y_recv, z_send, z_recv,
    az_send, az_recv, ay_send, ay_recv, ry_send, ry_recv, rz_send, rz_recv,
    out_send, out_recv, local_sem,
):
    t, h = lax.axis_index("tok"), lax.axis_index("head")
    y, z = lax.div(t, NZ), lax.rem(t, NZ)
    p, zq = lax.rem(z, 2), lax.div(z, 2)
    me = p * NH + h
    pair = t - p
    bits = [lax.rem(h, 2), lax.rem(lax.div(h, 2), 2), lax.div(h, 4), p]

    def remote(src, dst, send, recv, tok, head):
        return pltpu.make_async_remote_copy(
            src_ref=src, dst_ref=dst, send_sem=send, recv_sem=recv,
            device_id={"tok": tok, "head": head}, device_id_type=MESH,
        )

    def source(n):
        b = [1 - bit if n >> i & 1 else bit for i, bit in enumerate(bits)]
        head = b[0] + 2 * b[1] + 4 * b[2]
        return b[3] * NH + head, pair + b[3], head

    def tile_of(k):
        far = 1 - bits[2] if k & 1 else bits[2]
        other = 1 - p if k & 2 else p
        return 2 * other + far

    def y_peer(n):
        i = lax.rem(y + n, NY)
        return i, i * NZ + z

    def z_peer(n):
        i = lax.rem(zq + n, NQ)
        return i, y * NZ + 2 * i + p

    def span(index, size):
        return pl.ds(pl.multiple_of(index * size, size), size)

    own = span(me, ROWS)
    my_cols = span(2 * h + p, HD)
    copies = [
        pltpu.make_async_copy(rate_ref, rate_all, local_sem.at[0]),
        pltpu.make_async_copy(ids_ref, ids_in.at[p], local_sem.at[1]),
        pltpu.make_async_copy(table_ref.at[:, span(p, HD)], table, local_sem.at[2]),
        pltpu.make_async_copy(k_ref.at[:, my_cols], kb.at[own], local_sem.at[3]),
        pltpu.make_async_copy(v_ref.at[:, my_cols], vb.at[own], local_sem.at[4]),
        pltpu.make_async_copy(q_ref.at[:, my_cols], qb.at[own], local_sem.at[5]),
        pltpu.make_async_copy(w1_ref.at[p], w.at[0], local_sem.at[6]),
        pltpu.make_async_copy(w3_ref.at[p], w.at[1], local_sem.at[7]),
        pltpu.make_async_copy(w2_ref.at[p], w.at[2], local_sem.at[8]),
    ]
    for copy in copies:
        copy.start()

    barrier = pltpu.get_barrier_semaphore()
    for n in range(1, SRC):
        _, tok, head = source(n)
        pl.semaphore_signal(barrier, inc=1, device_id={"tok": tok, "head": head}, device_id_type=MESH)
    for n in range(1, NY):
        pl.semaphore_signal(barrier, inc=1, device_id={"tok": y_peer(n)[1], "head": h}, device_id_type=MESH)
    for n in range(1, NQ):
        pl.semaphore_signal(barrier, inc=1, device_id={"tok": z_peer(n)[1], "head": h}, device_id_type=MESH)

    copies[0].wait()
    eye = lax.broadcasted_iota(jnp.int32, (128, 128), 0) == lax.broadcasted_iota(jnp.int32, (128, 128), 1)
    by_head = rate_all[...].astype(F32)
    for head_no in range(2 * NH):
        rate_rows[head_no, :, :ROWS] = by_head[head_no : head_no + 1]
        rate_rows[head_no, :, ROWS:] = jnp.zeros((1, 128 - ROWS), F32)
    copies[1].wait()
    pl.semaphore_wait(barrier, SRC - 1 + NY - 1 + NQ - 1)

    id_copy = remote(ids_in.at[p], ids_in.at[p], id_send, id_recv, pair + 1 - p, h)
    id_copy.start()
    token_refs = ((k_ref, kb), (v_ref, vb), (q_ref, qb), (rate_rows, rb_in))

    def token_copy(kind, n):
        src, dst = token_refs[kind]
        s, tok, head = source(n)
        head_no = 2 * head + lax.div(s, NH)
        if kind == 3:
            a, b = src.at[head_no], dst.at[me]
        else:
            a, b = src.at[:, span(head_no, HD)], dst.at[own]
        copy = remote(a, b, tok_send.at[kind, s], tok_recv.at[kind, me], tok, head)
        copy.start()
        waiting.append(copy)

    def token_wait(kind, n):
        dst = token_refs[kind][1]
        s, tok, head = source(n)
        b = dst.at[s] if kind == 3 else dst.at[span(s, ROWS)]
        remote(b, b, tok_send.at[kind, s], tok_recv.at[kind, s], tok, head).wait_recv()

    waiting = [id_copy]
    order = (4, 8, 2, 6, 12, 10, 14, 5, 9, 3, 7, 13, 11, 15, 1)
    for n in order:
        token_copy(3, n)
    for n in order:
        token_copy(0, n)
    for n in order:
        token_copy(1, n)

    copies[2].wait()
    lane = lax.broadcasted_iota(jnp.int32, (TILE, 128), 1).astype(F32)

    def look(part):
        for group in range(4):
            row = ids_in[part, group : group + 1, :] if isinstance(part, int) else ids_in[part][group : group + 1, :]
            column = jnp.sum(jnp.where(eye, row.astype(F32), 0.0), axis=1, keepdims=True)
            idcol[pl.ds(group * 128, 128), :] = jnp.broadcast_to(column, (128, 128))

        def rows_of(i, _):
            ids = idcol[span(i, TILE), :]

            def some(j, total):
                first = (j * ITEM_TILE).astype(F32)
                hot = jnp.concatenate(
                    [jnp.where(ids - first == lane + 128.0 * b, 1.0, 0.0).astype(BF16) for b in range(ITEM_TILE // 128)],
                    axis=1,
                )
                return total + dot(hot, table[span(j, ITEM_TILE), :])

            found = lax.fori_loop(0, ITEMS // ITEM_TILE, some, jnp.zeros((TILE, HD), F32))
            looked[span(2 * part + i, TILE), :] = found.astype(BF16)
            return 0

        lax.fori_loop(0, 2, rows_of, 0)

    look(p)
    other_ids = ids_in.at[1 - p]
    remote(other_ids, other_ids, id_send, id_recv, pair + 1 - p, h).wait_recv()
    look(1 - p)

    for n in order:
        token_wait(3, n)
    for s in range(SRC):
        row = jnp.where(me == s, rate_rows[2 * h + p], rb_in[s])
        column = jnp.sum(jnp.where(eye[:ROWS], row, 0.0), axis=1, keepdims=True)
        rates[pl.ds(s * ROWS, ROWS), :] = jnp.broadcast_to(column, (ROWS, 128))

    split_at = bound_ref[0]
    counts = [split_at.astype(F32), (TOKENS - split_at).astype(F32)]
    first_row = pair * (TOKENS // (NY * NZ))

    def member(segment, start, size, width):
        positions = first_row + start + lax.broadcasted_iota(jnp.int32, (size, width), 0)
        return positions < split_at if segment == 0 else positions >= split_at

    sums = [
        jnp.sum(jnp.where(member(c, 0, LOCAL, 128), rates[...], 0.0), axis=0, keepdims=True) for c in range(2)
    ]
    rsum[...] = jnp.concatenate([jnp.broadcast_to(v, (8, 128)) for v in sums], axis=0)
    for n in range(1, NY):
        i, tok = y_peer(n)
        waiting.append(remote(rsum, rsum_y.at[y], ry_send.at[i], ry_recv.at[y], tok, h))
        waiting[-1].start()
    for copy in copies[3:]:
        copy.wait()

    def low(m):
        wl[m] = w[m].astype(BF16)

    for m in range(3):
        low(m)

    def queries(segment, i):
        rows = span(i, TILE)
        x = qb[rows, :]
        first_pre, third_pre = dot(x, wl[0]), dot(x, wl[1])
        act = (first_pre * sigmoid(first_pre) * third_pre).astype(BF16)
        applied = dot_cols(act, wl[2])
        if segment == 0:
            result[rows, :] = applied
        else:
            keep = member(1, i * TILE, TILE, HD)
            outb[rows, :] = jnp.where(keep, applied, result[rows, :]).astype(BF16)

    def forward(i):
        rows = span(i, TILE)
        key = kb[rows, :]
        first_pre, third_pre = dot(key, wl[0]), dot(key, wl[1])
        s = sigmoid(first_pre)
        silu = first_pre * s
        gate[rows, :] = silu
        slope[rows, :] = third_pre * (s * (1.0 + first_pre * (1.0 - s)))
        acts[rows, :] = (silu * third_pre).astype(BF16)

    def outward(c, i, first):
        rows = span(i, TILE)
        keep = member(c, i * TILE, TILE, 128)
        weighted = jnp.where(keep, rates[rows, :], 0.0)
        weighted = jnp.concatenate([weighted, weighted], axis=1)
        target = vb[rows, :].astype(F32) + looked[rows, :].astype(F32)
        upstream = (-weighted * target).astype(BF16)
        up[rows, :] = upstream
        add(2, dot_rows(upstream, acts[rows, :]), first)

    def backward(i, first):
        rows = span(i, TILE)
        key = kb[rows, :]
        back = dot(up[rows, :], wl[2])
        add(0, dot_rows(key, (back * slope[rows, :]).astype(BF16)), first)
        add(1, dot_rows(key, (back * gate[rows, :]).astype(BF16)), first)

    def add(m, part, first):
        for f in range(2):
            half = part[:, f * FT : (f + 1) * FT]
            if isinstance(first, bool):
                g[m, f] = half if first else half + g[m, f]
            else:
                g[m, f] = half + jnp.where(first, 0.0, g[m, f])

    my_y, my_z, mine = span(y, YR), span(zq, ZR), span(y * NQ + zq, ZR)

    chunks = ((2, 0), (2, 1), (0, 0), (0, 1), (1, 0), (1, 1))

    def send_y(c, k):
        m, f = chunks[k]
        gl[c, m, f] = g[m, f].astype(BF16)
        for n in range(1, NY):
            i, tok = y_peer(n)
            copy = remote(gl.at[c, m, f, span(i, YR)], ybuf.at[c, k, y], y_send.at[c, k, i], y_recv.at[c, k, y], tok, h)
            copy.start()
            waiting.append(copy)

    def reduce_y(c, k):
        m, f = chunks[k]
        total = g[m, f, my_y, :]
        for n in range(1, NY):
            i, tok = y_peer(n)
            b = ybuf.at[c, k, i]
            remote(b, b, y_send.at[c, k, i], y_recv.at[c, k, i], tok, h).wait_recv()
            total = total + ybuf[c, k, i].astype(F32)
        zown[k] = total
        zsend[c, k] = total.astype(BF16)
        for n in range(1, NQ):
            i, tok = z_peer(n)
            copy = remote(zsend.at[c, k, span(i, ZR)], zbuf.at[c, k, zq], z_send.at[c, k, i], z_recv.at[c, k, zq], tok, h)
            copy.start()
            waiting.append(copy)

    def reduce_z(c, k):
        m, f = chunks[k]
        total = zown[k, my_z, :]
        for n in range(1, NQ):
            i, tok = z_peer(n)
            b = zbuf.at[c, k, i]
            remote(b, b, z_send.at[c, k, i], z_recv.at[c, k, i], tok, h).wait_recv()
            total = total + zbuf[c, k, i].astype(F32)
        final[c, m, f, mine, :] = total.astype(BF16)
        for n in range(1, NQ):
            i, tok = z_peer(n)
            b = final.at[c, m, f, mine]
            copy = remote(b, b, az_send.at[c, k, i], az_recv.at[c, k, zq], tok, h)
            copy.start()
            waiting.append(copy)

    def gather_z(c, k):
        m, f = chunks[k]
        for n in range(1, NQ):
            i, tok = z_peer(n)
            b = final.at[c, m, f, span(y * NQ + i, ZR)]
            remote(b, b, az_send.at[c, k, i], az_recv.at[c, k, i], tok, h).wait_recv()
        for n in range(1, NY):
            i, tok = y_peer(n)
            b = final.at[c, m, f, my_y]
            copy = remote(b, b, ay_send.at[c, k, i], ay_recv.at[c, k, y], tok, h)
            copy.start()
            waiting.append(copy)

    def gather_y(c, k):
        m, f = chunks[k]
        for n in range(1, NY):
            i, tok = y_peer(n)
            b = final.at[c, m, f, span(i, YR)]
            remote(b, b, ay_send.at[c, k, i], ay_recv.at[c, k, i], tok, h).wait_recv()

    current = {}

    def iterate(c, m, number):
        if number == 0:
            x = jnp.concatenate([final[c, m, 0], final[c, m, 1]], axis=1).astype(F32)
            x = x / (jnp.sqrt(jnp.sum(x * x, keepdims=True)) + 1e-06)
        else:
            x = current[m]
        xl = x.astype(BF16)
        gram = dot_cols(xl, xl)
        gram_low = gram.astype(BF16)
        poly = C2 * gram + C3 * dot(gram_low, gram_low)
        current[m] = C1 * x + dot(poly.astype(BF16), xl)
        if number == NS_ITERS - 1:
            w[m] = w[m] - steps[c] * current[m]
            low(m)

    def rates_z():
        sums_y = rsum[...]
        for n in range(1, NY):
            i, tok = y_peer(n)
            remote(rsum, rsum_y.at[i], ry_send.at[i], ry_recv.at[i], tok, h).wait_recv()
            sums_y = sums_y + rsum_y[i]
        rsum_z[zq] = sums_y
        for n in range(1, NQ):
            i, tok = z_peer(n)
            waiting.append(remote(rsum_z.at[zq], rsum_z.at[zq], rz_send.at[i], rz_recv.at[zq], tok, h))
            waiting[-1].start()

    plan = (
        "y0 y1 y2 y3 z0 z1 y4 z2 y5 a0 z3 a1 z4 a2 z5 g0 a3 g1 n20 a4 n21 n22 a5 g2 g3 n00 n01 n02 g4 g5 n10 n11 n12"
    ).split()

    for c in range(2):
        if c == 0:
            for n in order:
                token_wait(0, n)

        def forward_of(i, _):
            forward(i)
            return 0

        lax.fori_loop(0, LOCAL // TILE, forward_of, 0)
        if c == 0:
            for n in order:
                token_wait(1, n)

        def outward_of(i, _, c=c):
            outward(c, i, i == 0)
            return 0

        lax.fori_loop(0, LOCAL // TILE, outward_of, 0)
        send_y(c, 0)
        send_y(c, 1)

        def backward_of(i, _):
            backward(i, i == 0)
            return 0

        lax.fori_loop(0, LOCAL // TILE, backward_of, 0)
        for k in range(2, 6):
            send_y(c, k)
        if c == 0:
            rates_z()
        for word in plan:
            kind, index = word[0], int(word[1])
            if c == 1 and word == "z0":

                def query_of(i, _):
                    queries(0, i)
                    return 0

                lax.fori_loop(0, LOCAL // TILE, query_of, 0)
            if c == 0 and word == "g0":
                for n in order:
                    token_copy(2, n)
            if kind == "n":
                if c == 0 and word == "n20":
                    for n in range(1, NQ):
                        i, tok = z_peer(n)
                        remote(rsum_z.at[i], rsum_z.at[i], rz_send.at[i], rz_recv.at[i], tok, h).wait_recv()
                    sums_all = rsum_z[0] + rsum_z[1] + rsum_z[2] + rsum_z[3]
                    steps = [sums_all[8 * i : 8 * i + 1, 0:1] / counts[i] for i in range(2)]
                iterate(c, index, int(word[2]))
            else:
                {"y": reduce_y, "z": reduce_z, "a": gather_z, "g": gather_y}[kind](c, index)
        if c == 0:
            for n in order:
                token_wait(2, n)

    for k in (3, 1, 2, 0):
        queries(1, tile_of(k))
        for n in range(4 * k, 4 * k + 4):
            if n:
                s, tok, head = source(n)
                copy = remote(outb.at[span(s, ROWS)], out_ref.at[:, my_cols], out_send.at[s], out_recv.at[me], tok, head)
                copy.start()
                waiting.append(copy)
    mine_copy = pltpu.make_async_copy(outb.at[own], out_ref.at[:, my_cols], local_sem.at[9])
    mine_copy.start()
    for copy in waiting:
        copy.wait_send()
    for n in range(1, SRC):
        s, tok, head = source(n)
        b = out_ref.at[:, span(2 * head + lax.div(s, NH), HD)]
        remote(b, b, out_send.at[s], out_recv.at[s], tok, head).wait_recv()
    mine_copy.wait()


def shards(queries, keys, values, rates, item_ids, boundary, item_table, w_first, w_third, w_out):
    ids = item_ids.reshape(4, 128)
    pin = lambda x: pltpu.with_memory_space_constraint(x, pltpu.HBM)
    hbm = pl.BlockSpec(memory_space=pltpu.HBM)
    dma = pltpu.SemaphoreType.DMA
    return pl.pallas_call(
        kernel,
        out_shape=jax.ShapeDtypeStruct((ROWS, D), BF16),
        in_specs=[hbm, hbm, hbm, hbm, hbm, pl.BlockSpec(memory_space=pltpu.SMEM), hbm, hbm, hbm, hbm],
        out_specs=pl.BlockSpec(memory_space=pl.ANY),
        scratch_shapes=[
            pltpu.VMEM((LOCAL, HD), BF16),
            pltpu.VMEM((LOCAL, HD), BF16),
            pltpu.VMEM((LOCAL, HD), BF16),
            pltpu.VMEM((2 * NH, ROWS), BF16),
            pltpu.VMEM((2 * NH, 1, 128), F32),
            pltpu.VMEM((SRC, 1, 128), F32),
            pltpu.VMEM((2, 4, 128), jnp.int32),
            pltpu.VMEM((ITEMS, HD), BF16),
            pltpu.VMEM((3, HD, FH), F32),
            pltpu.VMEM((3, HD, FH), BF16),
            pltpu.VMEM((LOCAL, 128), F32),
            pltpu.VMEM((512, 128), F32),
            pltpu.VMEM((LOCAL, HD), BF16),
            pltpu.VMEM((LOCAL, HD), BF16),
            pltpu.VMEM((LOCAL, FH), BF16),
            pltpu.VMEM((LOCAL, FH), F32),
            pltpu.VMEM((LOCAL, FH), F32),
            pltpu.VMEM((3, 2, HD, FT), F32),
            pltpu.VMEM((2, 3, 2, HD, FT), BF16),
            pltpu.VMEM((2, 6, NY, YR, FT), BF16),
            pltpu.VMEM((6, YR, FT), F32),
            pltpu.VMEM((2, 6, YR, FT), BF16),
            pltpu.VMEM((2, 6, NQ, ZR, FT), BF16),
            pltpu.VMEM((2, 3, 2, HD, FT), BF16),
            pltpu.VMEM((16, 128), F32),
            pltpu.VMEM((NY, 16, 128), F32),
            pltpu.VMEM((NQ, 16, 128), F32),
            pltpu.VMEM((LOCAL, HD), F32),
            pltpu.VMEM((LOCAL, HD), BF16),
            dma((4, SRC)), dma((4, SRC)), dma, dma,
            dma((2, 6, NY)), dma((2, 6, NY)), dma((2, 6, NQ)), dma((2, 6, NQ)),
            dma((2, 6, NQ)), dma((2, 6, NQ)), dma((2, 6, NY)), dma((2, 6, NY)),
            dma((NY,)), dma((NY,)), dma((NQ,)), dma((NQ,)),
            dma((SRC,)), dma((SRC,)), dma((10,)),
        ],
        compiler_params=pltpu.CompilerParams(
            collective_id=0, has_side_effects=True, vmem_limit_bytes=40 * 1024 * 1024
        ),
        name="layer",
    )(*map(pin, (queries, keys, values, rates.T, ids)), boundary, *map(pin, (item_table, w_first, w_third, w_out)))


def solution(mesh):
    in_specs = (
        P(("tok", "head"), None),
        P(("tok", "head"), None),
        P(("tok", "head"), None),
        P(("tok", "head"), None),
        P("tok"),
        P(),
        P(None, "head"),
        P("head", None, None),
        P("head", None, None),
        P("head", None, None),
    )
    out_specs = P(("tok", "head"), None)
    return jax.shard_map(shards, mesh=mesh, in_specs=in_specs, out_specs=out_specs, check_vma=False)
```

```python
import functools

import jax
import jax.numpy as jnp
from jax import lax
from jax.experimental import pallas as pl
from jax.experimental.pallas import tpu as pltpu
from jax.sharding import PartitionSpec as P

MESH = pl.DeviceIdType.MESH
F32, BF16 = jnp.float32, jnp.bfloat16

NY, NZ = 4, 8
NQ = NZ // 2
NH = 8
ROWS, D, HD, FH, ITEMS, TOKENS = 64, 4096, 256, 512, 4096, 16384
SRC = 2 * NH
LOCAL = SRC * ROWS
YR, ZR = HD // NY, HD // NY // NQ
NS_ITERS = 3
C1, C2, C3 = 3.4445, -4.775, 2.0315
TILE = 256
FT = FH // 2
FT = FH // 2
FT = FH // 2
FT = FH // 2
FT = FH // 2
FT = FH // 2
FT = FH // 2
FT = FH // 2
FT = FH // 2
FT = FH // 2
FT = FH // 2
FT = FH // 2
FT = FH // 2
FT = FH // 2
ITEM_TILE = 512


def dot(a, b):
    return jnp.dot(a, b, preferred_element_type=F32)


def dot_rows(a, b):
    return lax.dot_general(a, b, (((0,), (0,)), ((), ())), preferred_element_type=F32)


def dot_cols(a, b):
    return lax.dot_general(a, b, (((1,), (1,)), ((), ())), preferred_element_type=F32)


def sigmoid(u):
    return 0.5 * jnp.tanh(0.5 * u) + 0.5


def kernel(
    q_ref, k_ref, v_ref, rate_ref, ids_ref, bound_ref, table_ref, w1_ref, w3_ref, w2_ref,
    out_ref,
    kb, vb, qb, rate_all, rate_rows, rb_in, ids_in, table, w, wl, rates, idcol, looked, up, acts, gate, slope, g, gl,
    ybuf, zown, zsend, zbuf, final, rsum, rsum_y, rsum_z, result, outb,
    tok_send, tok_recv, id_send, id_recv, part_send, part_recv, rsum_send, rsum_recv,
    out_send, out_recv, local_sem,
):
    t, h = lax.axis_index("tok"), lax.axis_index("head")
    y, z = lax.div(t, NZ), lax.rem(t, NZ)
    p, zq = lax.rem(z, 2), lax.div(z, 2)
    bits = [lax.rem(h, 2), lax.rem(lax.div(h, 2), 2), lax.div(h, 4)]
    next_z, last_z = y * NZ + lax.rem(z + 1, NZ), y * NZ + lax.rem(z + NZ - 1, NZ)
    other_tok = last_z + bits[2] * (next_z - last_z)

    def remote(src, dst, send, recv, tok, head):
        return pltpu.make_async_remote_copy(
            src_ref=src, dst_ref=dst, send_sem=send, recv_sem=recv,
            device_id={"tok": tok, "head": head}, device_id_type=MESH,
        )

    def head_at(n):
        b = [1 - bit if n >> i & 1 else bit for i, bit in enumerate(bits)]
        return b[0] + 2 * b[1] + 4 * b[2], b[2]

    def target(n):
        head, _ = head_at(n % NH)
        return (t, head, 2 * head + p, h) if n < NH else (other_tok, head, 2 * head + 1 - p, NH + h)

    def origin(n):
        head, far = head_at(n % NH)
        return (t, head, head) if n < NH else (next_z + far * (last_z - next_z), head, NH + head)

    def y_peer(n):
        i = lax.rem(y + n, NY)
        return i, i * NZ + z

    def z_peer(n):
        i = lax.rem(zq + n, NQ)
        return i, y * NZ + 2 * i + p

    def span(index, size):
        return pl.ds(pl.multiple_of(index * size, size), size)

    barrier = pltpu.get_barrier_semaphore()
    greeted = [target(n)[:2] for n in range(1, SRC)]
    greeted += [(last_z + next_z - other_tok, (NH // 2) * bits[2] + j) for j in range(NH // 2)]
    for tok, head in greeted:
        pl.semaphore_signal(barrier, inc=1, device_id={"tok": tok, "head": head}, device_id_type=MESH)
    for n in range(1, NY):
        pl.semaphore_signal(barrier, inc=1, device_id={"tok": y_peer(n)[1], "head": h}, device_id_type=MESH)
    for n in range(1, NQ):
        pl.semaphore_signal(barrier, inc=1, device_id={"tok": z_peer(n)[1], "head": h}, device_id_type=MESH)

    own = span(h, ROWS)
    my_cols = span(2 * h + p, HD)
    copies = [
        pltpu.make_async_copy(rate_ref, rate_all, local_sem.at[0]),
        pltpu.make_async_copy(ids_ref, ids_in.at[0], local_sem.at[1]),
        pltpu.make_async_copy(table_ref.at[:, span(p, HD)], table, local_sem.at[2]),
        pltpu.make_async_copy(k_ref.at[:, my_cols], kb.at[own], local_sem.at[3]),
        pltpu.make_async_copy(v_ref.at[:, my_cols], vb.at[own], local_sem.at[4]),
        pltpu.make_async_copy(q_ref.at[:, my_cols], qb.at[own], local_sem.at[5]),
    ]
    weight_copies = [
        pltpu.make_async_copy(ref.at[p], w.at[m], local_sem.at[6]) for m, ref in enumerate((w1_ref, w3_ref, w2_ref))
    ]
    for copy in copies + weight_copies:
        copy.start()

    copies[0].wait()
    eye = lax.broadcasted_iota(jnp.int32, (128, 128), 0) == lax.broadcasted_iota(jnp.int32, (128, 128), 1)
    by_head = rate_all[...].astype(F32)
    for head_no in range(2 * NH):
        rate_rows[head_no, :, :ROWS] = by_head[head_no : head_no + 1]
        rate_rows[head_no, :, ROWS:] = jnp.zeros((1, 128 - ROWS), F32)
    copies[1].wait()
    pl.semaphore_wait(barrier, len(greeted) + NY - 1 + NQ - 1)

    for slot, tok in ((2, next_z), (1, last_z)):
        remote(ids_in.at[0], ids_in.at[slot], id_send, id_recv.at[slot - 1], tok, h).start()
    token_refs = ((k_ref, kb), (v_ref, vb), (q_ref, qb), (rate_rows, rb_in))

    def token_copy(kind, n):
        src, dst = token_refs[kind]
        tok, head, head_no, slot = target(n)
        if kind == 3:
            a, b = src.at[head_no], dst.at[slot]
        else:
            a, b = src.at[:, span(head_no, HD)], dst.at[span(slot, ROWS)]
        remote(a, b, tok_send.at[kind], tok_recv.at[kind], tok, head).start()

    def all_but_one(kind):
        dst = token_refs[kind][1]
        return dst.at[pl.ds(0, SRC - 1)] if kind == 3 else dst.at[pl.ds(0, (SRC - 1) * ROWS)]

    def token_wait(kind):
        b = all_but_one(kind)
        remote(b, b, tok_send.at[kind], tok_recv.at[kind], t, h).wait_recv()

    order = (12, 14, 10, 13, 15, 11, 4, 6, 2, 5, 7, 3, 8, 9, 1)
    for n in order:
        token_copy(3, n)
    for n in order:
        token_copy(0, n)
    for n in order:
        token_copy(1, n)

    copies[2].wait()
    lane = lax.broadcasted_iota(jnp.int32, (TILE, 128), 1).astype(F32)

    def look(part, slots):
        for group, slot in enumerate(slots):
            row = ids_in[slot, group : group + 1, :]
            column = jnp.sum(jnp.where(eye, row.astype(F32), 0.0), axis=1, keepdims=True)
            idcol[pl.ds(group * 128, 128), :] = jnp.broadcast_to(column, (128, 128))

        def rows_of(i, _):
            ids = idcol[span(i, TILE), :]

            def some(j, total):
                first = (j * ITEM_TILE).astype(F32)
                hot = jnp.concatenate(
                    [jnp.where(ids - first == lane + 128.0 * b, 1.0, 0.0).astype(BF16) for b in range(ITEM_TILE // 128)],
                    axis=1,
                )
                return total + dot(hot, table[span(j, ITEM_TILE), :])

            found = lax.fori_loop(0, ITEMS // ITEM_TILE, some, jnp.zeros((TILE, HD), F32))
            looked[span(2 * part + i, TILE), :] = found.astype(BF16)
            return 0

        lax.fori_loop(0, 2, rows_of, 0)

    look(0, (0, 0, 0, 0))
    for slot in (1, 2):
        remote(ids_in.at[slot], ids_in.at[slot], id_send, id_recv.at[slot - 1], t, h).wait_recv()
    look(1, (1, 1, 2, 2))

    token_wait(3)
    for s in range(SRC):
        row = jnp.where(h == s, rate_rows[2 * h + p], rb_in[s])
        column = jnp.sum(jnp.where(eye[:ROWS], row, 0.0), axis=1, keepdims=True)
        rates[pl.ds(s * ROWS, ROWS), :] = jnp.broadcast_to(column, (ROWS, 128))

    split_at = bound_ref[0]
    counts = [split_at.astype(F32), (TOKENS - split_at).astype(F32)]
    block = TOKENS // (NY * NZ)
    starts = (t * block, t * block + TILE, next_z * block, last_z * block + TILE)

    def member(segment, start, width):
        positions = start + lax.broadcasted_iota(jnp.int32, (TILE, width), 0)
        return positions < split_at if segment == 0 else positions >= split_at

    def start_of(i):
        start = starts[3]
        for j in (2, 1, 0):
            start = jnp.where(i == j, starts[j], start)
        return start

    def weighted_sum(c):
        parts = [jnp.where(member(c, starts[j], 128), rates[pl.ds(j * TILE, TILE), :], 0.0) for j in range(4)]
        return jnp.sum(parts[0] + parts[1] + parts[2] + parts[3], axis=0, keepdims=True)

    sums = [weighted_sum(c) for c in range(2)]
    rsum[...] = jnp.concatenate([jnp.broadcast_to(v, (8, 128)) for v in sums], axis=0)
    for n in range(1, NY):
        i, tok = y_peer(n)
        remote(rsum, rsum_y.at[y], rsum_send.at[0], rsum_recv.at[0], tok, h).start()
    for copy in copies[3:]:
        copy.wait()
    pltpu.make_async_copy(w, w, local_sem.at[6]).wait()

    def low(m):
        wl[m] = w[m].astype(BF16)

    for m in range(3):
        low(m)

    def queries(segment, i):
        rows = span(i, TILE)
        x = qb[rows, :]
        first_pre, third_pre = dot(x, wl[0]), dot(x, wl[1])
        act = (first_pre * sigmoid(first_pre) * third_pre).astype(BF16)
        applied = dot_cols(act, wl[2])
        if segment == 0:
            result[rows, :] = applied
        else:
            keep = member(1, start_of(i), HD)
            outb[rows, :] = jnp.where(keep, applied, result[rows, :]).astype(BF16)

    def forward(i, f):
        rows, cols = span(i, TILE), pl.ds(f * FT, FT)
        key = kb[rows, :]
        first_pre, third_pre = dot(key, wl[0, :, cols]), dot(key, wl[1, :, cols])
        s = sigmoid(first_pre)
        silu = first_pre * s
        gate[rows, cols] = silu
        slope[rows, cols] = third_pre * (s * (1.0 + first_pre * (1.0 - s)))
        acts[rows, cols] = (silu * third_pre).astype(BF16)

    def outward(c, i, f):
        rows = span(i, TILE)
        if f == 0:
            keep = member(c, starts[i], 128)
            weighted = jnp.where(keep, rates[rows, :], 0.0)
            weighted = jnp.concatenate([weighted, weighted], axis=1)
            target = vb[rows, :].astype(F32) + looked[rows, :].astype(F32)
            up[rows, :] = (-weighted * target).astype(BF16)
        part = dot_rows(up[rows, :], acts[rows, pl.ds(f * FT, FT)])
        g[2, f] = part if i == 0 else part + g[2, f]

    def backward(i, first):
        rows = span(i, TILE)
        key = kb[rows, :]
        back = dot(up[rows, :], wl[2])
        add(0, dot_rows(key, (back * slope[rows, :]).astype(BF16)), first)
        add(1, dot_rows(key, (back * gate[rows, :]).astype(BF16)), first)

    def add(m, part, first):
        for f in range(2):
            half = part[:, f * FT : (f + 1) * FT]
            if isinstance(first, bool):
                g[m, f] = half if first else half + g[m, f]
            else:
                g[m, f] = half + jnp.where(first, 0.0, g[m, f])

    chunks = ((2, 0), (2, 1), (0, 0), (0, 1), (1, 0), (1, 1))
    stages = (((y, y_peer), (zq, z_peer)), ((zq, z_peer), (y, y_peer)))

    def stages_of(k):
        return stages[1 if k == 5 else 0]

    def part_wait(k, stage, b):
        remote(b, b, part_send.at[stage], part_recv.at[k, stage], t, h).wait_recv()

    def send_first(c, k):
        (m, f), (here, peer) = chunks[k], stages_of(k)[0]
        gl[c, m, f] = g[m, f].astype(BF16)
        for n in range(1, NY):
            i, tok = peer(n)
            remote(gl.at[c, m, f, span(i, YR)], ybuf.at[c, k, here], part_send.at[0], part_recv.at[k, 0], tok, h).start()

    def reduce_first(c, k):
        (m, f), ((first, peer1), (second, peer2)) = chunks[k], stages_of(k)
        total = g[m, f, span(first, YR), :]
        part_wait(k, 0, ybuf.at[c, k, pl.ds(0, NY - 1)])
        for n in range(1, NY):
            total = total + ybuf[c, k, peer1(n)[0]].astype(F32)
        zown[k] = total
        zsend[c, k] = total.astype(BF16)
        for n in range(1, NQ):
            i, tok = peer2(n)
            remote(zsend.at[c, k, span(i, ZR)], zbuf.at[c, k, second], part_send.at[1], part_recv.at[k, 1], tok, h).start()

    def reduce_second(c, k):
        (m, f), ((first, _), (second, peer2)) = chunks[k], stages_of(k)
        total = zown[k, span(second, ZR), :]
        part_wait(k, 1, zbuf.at[c, k, pl.ds(0, NQ - 1)])
        for n in range(1, NQ):
            total = total + zbuf[c, k, peer2(n)[0]].astype(F32)
        mine = span(first * NQ + second, ZR)
        final[c, m, f, mine, :] = total.astype(BF16)
        for n in range(1, NQ):
            i, tok = peer2(n)
            b = final.at[c, m, f, mine]
            remote(b, b, part_send.at[2], part_recv.at[k, 2], tok, h).start()

    def gather_second(c, k):
        (m, f), (first, peer1) = chunks[k], stages_of(k)[0]
        part_wait(k, 2, final.at[c, m, f, pl.ds(0, (NQ - 1) * ZR)])
        for n in range(1, NY):
            i, tok = peer1(n)
            b = final.at[c, m, f, span(first, YR)]
            remote(b, b, part_send.at[3], part_recv.at[k, 3], tok, h).start()

    def gather_first(c, k):
        m, f = chunks[k]
        part_wait(k, 3, final.at[c, m, f, pl.ds(0, (NY - 1) * YR)])

    current = {}
    eye_hd = lax.broadcasted_iota(jnp.int32, (HD, HD), 0) == lax.broadcasted_iota(jnp.int32, (HD, HD), 1)

    def iterate(c, m, number):
        if number == 0:
            x = jnp.concatenate([final[c, m, 0], final[c, m, 1]], axis=1)
        else:
            x = current[m]
        xl = x.astype(BF16)
        gram = dot_cols(xl, xl)
        if number == 0:
            scale = 1.0 / (jnp.sqrt(jnp.sum(jnp.where(eye_hd, gram, 0.0), keepdims=True)) + 1e-06)
            gram = gram * (scale * scale)
        gram_low = gram.astype(BF16)
        poly = C2 * gram + C3 * dot(gram_low, gram_low)
        x = C1 * x.astype(F32) + dot(poly.astype(BF16), xl)
        current[m] = x * scale if number == 0 else x
        if number == NS_ITERS - 1:
            w[m] = w[m] - steps[c] * current[m]
            low(m)

    def rates_z():
        sums_y = rsum[...]
        b = rsum_y.at[pl.ds(0, NY - 1)]
        remote(b, b, rsum_send.at[0], rsum_recv.at[0], t, h).wait()
        for n in range(1, NY):
            sums_y = sums_y + rsum_y[y_peer(n)[0]]
        rsum_z[zq] = sums_y
        for n in range(1, NQ):
            i, tok = z_peer(n)
            remote(rsum_z.at[zq], rsum_z.at[zq], rsum_send.at[1], rsum_recv.at[1], tok, h).start()

    plan = (
        "q", "q", "q", "y0", "y1", "q", "y2", "y3", "z0", "y5",
        "y4", "z1", "z2", "z5", "z3", "a0", "z4", "a1", "a2", "a5",
        "a3", "g0", "a4", "g1", "n20", "n21", "n22", "g2", "g3", "n00",
        "n01", "n02", "g5", "g4", "n10", "n11", "n12",
    )

    for c in range(2):
        if c == 0:
            token_wait(0)
            for f in range(2):
                for i in range(LOCAL // TILE):
                    forward(i, f)
            token_wait(1)
        for f in range(2):
            for i in range(LOCAL // TILE):
                if c == 1:
                    forward(i, f)
            for i in range(LOCAL // TILE):
                outward(c, i, f)
            send_first(c, f)

        def backward_of(i, _):
            backward(i, i == 0)
            return 0

        lax.fori_loop(0, LOCAL // TILE, backward_of, 0, unroll=True)
        for k in (5, 2, 3, 4):
            send_first(c, k)
        if c == 0:
            rates_z()
        asked = 0
        for word in plan:
            kind, index = word[0], int(word[1:2] or 0)
            if kind == "q":
                if c == 1:
                    queries(0, asked)
                    asked += 1
                continue
            if c == 0 and word == "g0":
                for n in order:
                    token_copy(2, n)
            if kind == "n":
                if c == 0 and word == "n20":
                    b = rsum_z.at[pl.ds(0, NQ - 1)]
                    remote(b, b, rsum_send.at[1], rsum_recv.at[1], t, h).wait()
                    sums_all = rsum_z[0] + rsum_z[1] + rsum_z[2] + rsum_z[3]
                    steps = [sums_all[8 * i : 8 * i + 1, 0:1] / counts[i] for i in range(2)]
                iterate(c, index, int(word[2]))
            elif kind == "p":
                for number in range(NS_ITERS):
                    for m in range(2):
                        iterate(c, m, number)
            else:
                {"y": reduce_first, "z": reduce_second, "a": gather_second, "g": gather_first}[kind](c, index)
        if c == 0:
            token_wait(2)

    for k in (3, 2, 1, 0):
        queries(1, k if k > 1 else 1 - bits[2] if k else bits[2])
        for j in range(4):
            if k > 1:
                tok, head, slot = (last_z, j + 4, NH + 4 + j) if k == 3 else (next_z, j, NH + j)
            elif k or j:
                tok, head, slot = origin(4 * k + j)
            else:
                continue
            remote(outb.at[span(slot, ROWS)], out_ref.at[:, my_cols], out_send, out_recv, tok, head).start()
    mine_copy = pltpu.make_async_copy(outb.at[own], out_ref.at[:, my_cols], local_sem.at[7])
    mine_copy.start()
    for kind in range(4):
        b = all_but_one(kind)
        remote(b, b, tok_send.at[kind], tok_recv.at[kind], t, h).wait_send()
    remote(ids_in.at[pl.ds(0, 2)], ids_in.at[pl.ds(0, 2)], id_send, id_recv.at[0], t, h).wait_send()
    for stage in range(4):
        b = zsend.at[:, :, pl.ds(0, (NQ - 1) * ZR)] if stage in (1, 2) else gl.at[:, :, :, pl.ds(0, (NY - 1) * YR)]
        remote(b, b, part_send.at[stage], part_recv.at[0, stage], t, h).wait_send()
    b = out_ref.at[:, pl.ds(0, D - HD)]
    remote(b, b, out_send, out_recv, t, h).wait()
    mine_copy.wait()


def shards(queries, keys, values, rates, item_ids, boundary, item_table, w_first, w_third, w_out):
    ids = item_ids.reshape(4, 128)
    pin = lambda x: pltpu.with_memory_space_constraint(x, pltpu.HBM)
    hbm = pl.BlockSpec(memory_space=pltpu.HBM)
    dma = pltpu.SemaphoreType.DMA
    return pl.pallas_call(
        kernel,
        out_shape=jax.ShapeDtypeStruct((ROWS, D), BF16),
        in_specs=[hbm, hbm, hbm, hbm, hbm, pl.BlockSpec(memory_space=pltpu.SMEM), hbm, hbm, hbm, hbm],
        out_specs=pl.BlockSpec(memory_space=pl.ANY),
        scratch_shapes=[
            pltpu.VMEM((LOCAL, HD), BF16),
            pltpu.VMEM((LOCAL, HD), BF16),
            pltpu.VMEM((LOCAL, HD), BF16),
            pltpu.VMEM((2 * NH, ROWS), BF16),
            pltpu.VMEM((2 * NH, 1, 128), F32),
            pltpu.VMEM((SRC, 1, 128), F32),
            pltpu.VMEM((3, 4, 128), jnp.int32),
            pltpu.VMEM((ITEMS, HD), BF16),
            pltpu.VMEM((3, HD, FH), F32),
            pltpu.VMEM((3, HD, FH), BF16),
            pltpu.VMEM((LOCAL, 128), F32),
            pltpu.VMEM((512, 128), F32),
            pltpu.VMEM((LOCAL, HD), BF16),
            pltpu.VMEM((LOCAL, HD), BF16),
            pltpu.VMEM((LOCAL, FH), BF16),
            pltpu.VMEM((LOCAL, FH), F32),
            pltpu.VMEM((LOCAL, FH), F32),
            pltpu.VMEM((3, 2, HD, FT), F32),
            pltpu.VMEM((2, 3, 2, HD, FT), BF16),
            pltpu.VMEM((2, 6, NY, YR, FT), BF16),
            pltpu.VMEM((6, YR, FT), F32),
            pltpu.VMEM((2, 6, YR, FT), BF16),
            pltpu.VMEM((2, 6, NQ, ZR, FT), BF16),
            pltpu.VMEM((2, 3, 2, HD, FT), BF16),
            pltpu.VMEM((16, 128), F32),
            pltpu.VMEM((NY, 16, 128), F32),
            pltpu.VMEM((NQ, 16, 128), F32),
            pltpu.VMEM((LOCAL, HD), F32),
            pltpu.VMEM((LOCAL, HD), BF16),
            dma((4,)), dma((4,)), dma, dma((2,)), dma((4,)), dma((6, 4)), dma((2,)), dma((2,)),
            dma, dma, dma((8,)),
        ],
        compiler_params=pltpu.CompilerParams(
            collective_id=0, has_side_effects=True, vmem_limit_bytes=40 * 1024 * 1024
        ),
        name="layer",
    )(*map(pin, (queries, keys, values, rates.T, ids)), boundary, *map(pin, (item_table, w_first, w_third, w_out)))


def solution(mesh):
    in_specs = (
        P(("tok", "head"), None),
        P(("tok", "head"), None),
        P(("tok", "head"), None),
        P(("tok", "head"), None),
        P("tok"),
        P(),
        P(None, "head"),
        P("head", None, None),
        P("head", None, None),
        P("head", None, None),
    )
    out_specs = P(("tok", "head"), None)
    return jax.shard_map(shards, mesh=mesh, in_specs=in_specs, out_specs=out_specs, check_vma=False)
```

```python
import functools

import jax
import jax.numpy as jnp
from jax import lax
from jax.experimental import pallas as pl
from jax.experimental.pallas import tpu as pltpu
from jax.sharding import PartitionSpec as P

MESH = pl.DeviceIdType.MESH
F32, BF16 = jnp.float32, jnp.bfloat16

NY, NZ = 4, 8
NQ = NZ // 2
NH = 8
ROWS, D, HD, FH, ITEMS, TOKENS = 64, 4096, 256, 512, 4096, 16384
SRC = 2 * NH
LOCAL = SRC * ROWS
YR, ZR = HD // NY, HD // NY // NQ
NS_ITERS = 3
C1, C2, C3 = 3.4445, -4.775, 2.0315
TILE = 256
FT = FH // 2
FT = FH // 2
FT = FH // 2
FT = FH // 2
FT = FH // 2
FT = FH // 2
FT = FH // 2
FT = FH // 2
FT = FH // 2
FT = FH // 2
FT = FH // 2
FT = FH // 2
FT = FH // 2
FT = FH // 2
FT = FH // 2
ITEM_TILE = 512


def dot(a, b):
    return jnp.dot(a, b, preferred_element_type=F32)


def dot_rows(a, b):
    return lax.dot_general(a, b, (((0,), (0,)), ((), ())), preferred_element_type=F32)


def dot_cols(a, b):
    return lax.dot_general(a, b, (((1,), (1,)), ((), ())), preferred_element_type=F32)


def sigmoid(u):
    return 0.5 * jnp.tanh(0.5 * u) + 0.5


def kernel(
    q_ref, k_ref, v_ref, rate_ref, ids_ref, bound_ref, table_ref, w1_ref, w3_ref, w2_ref,
    out_ref,
    kb, vb, qb, rate_all, rate_rows, rb_in, ids_in, table, w, wl, rates, idcol, looked, up, acts, gate, slope, g, gl,
    ybuf, zown, zsend, zbuf, final, rsum, rsum_y, rsum_z, result, outb,
    tok_send, tok_recv, id_send, id_recv, part_send, part_recv, rsum_send, rsum_recv,
    out_send, out_recv, local_sem,
):
    t, h = lax.axis_index("tok"), lax.axis_index("head")
    y, z = lax.div(t, NZ), lax.rem(t, NZ)
    p, zq = lax.rem(z, 2), lax.div(z, 2)
    bits = [lax.rem(h, 2), lax.rem(lax.div(h, 2), 2), lax.div(h, 4)]
    next_z, last_z = y * NZ + lax.rem(z + 1, NZ), y * NZ + lax.rem(z + NZ - 1, NZ)
    other_tok = last_z + bits[2] * (next_z - last_z)

    def remote(src, dst, send, recv, tok, head):
        return pltpu.make_async_remote_copy(
            src_ref=src, dst_ref=dst, send_sem=send, recv_sem=recv,
            device_id={"tok": tok, "head": head}, device_id_type=MESH,
        )

    def head_at(n):
        b = [1 - bit if n >> i & 1 else bit for i, bit in enumerate(bits)]
        return b[0] + 2 * b[1] + 4 * b[2], b[2]

    def target(n):
        head, _ = head_at(n % NH)
        return (t, head, 2 * head + p, h) if n < NH else (other_tok, head, 2 * head + 1 - p, NH + h)

    def origin(n):
        head, far = head_at(n % NH)
        return (t, head, head) if n < NH else (next_z + far * (last_z - next_z), head, NH + head)

    def y_peer(n):
        i = lax.rem(y + n, NY)
        return i, i * NZ + z

    def z_peer(n):
        i = lax.rem(zq + n, NQ)
        return i, y * NZ + 2 * i + p

    def span(index, size):
        return pl.ds(pl.multiple_of(index * size, size), size)

    barrier = pltpu.get_barrier_semaphore()
    greeted = [target(n)[:2] for n in range(1, SRC)]
    greeted += [(last_z + next_z - other_tok, (NH // 2) * bits[2] + j) for j in range(NH // 2)]
    for tok, head in greeted:
        pl.semaphore_signal(barrier, inc=1, device_id={"tok": tok, "head": head}, device_id_type=MESH)
    for n in range(1, NY):
        pl.semaphore_signal(barrier, inc=1, device_id={"tok": y_peer(n)[1], "head": h}, device_id_type=MESH)
    for n in range(1, NQ):
        pl.semaphore_signal(barrier, inc=1, device_id={"tok": z_peer(n)[1], "head": h}, device_id_type=MESH)

    own = span(h, ROWS)
    my_cols = span(2 * h + p, HD)
    copies = [
        pltpu.make_async_copy(rate_ref, rate_all, local_sem.at[0]),
        pltpu.make_async_copy(ids_ref, ids_in.at[0], local_sem.at[1]),
        pltpu.make_async_copy(table_ref.at[:, span(p, HD)], table, local_sem.at[2]),
        pltpu.make_async_copy(k_ref.at[:, my_cols], kb.at[own], local_sem.at[3]),
        pltpu.make_async_copy(v_ref.at[:, my_cols], vb.at[own], local_sem.at[4]),
        pltpu.make_async_copy(q_ref.at[:, my_cols], qb.at[own], local_sem.at[5]),
    ]
    weight_copies = [
        pltpu.make_async_copy(ref.at[p], w.at[m], local_sem.at[6]) for m, ref in enumerate((w1_ref, w3_ref, w2_ref))
    ]
    for copy in copies + weight_copies:
        copy.start()

    pl.semaphore_wait(barrier, len(greeted) + NY - 1 + NQ - 1)

    for slot, tok in ((2, next_z), (1, last_z)):
        remote(ids_ref, ids_in.at[slot], id_send, id_recv.at[slot - 1], tok, h).start()
    token_refs = ((k_ref, kb), (v_ref, vb), (q_ref, qb), (rate_rows, rb_in))

    def token_copy(kind, n):
        src, dst = token_refs[kind]
        tok, head, head_no, slot = target(n)
        if kind == 3:
            a, b = src.at[head_no], dst.at[slot]
        else:
            a, b = src.at[:, span(head_no, HD)], dst.at[span(slot, ROWS)]
        remote(a, b, tok_send.at[kind], tok_recv.at[kind], tok, head).start()

    def all_but_one(kind):
        dst = token_refs[kind][1]
        return dst.at[pl.ds(0, SRC - 1)] if kind == 3 else dst.at[pl.ds(0, (SRC - 1) * ROWS)]

    def token_wait(kind):
        b = all_but_one(kind)
        remote(b, b, tok_send.at[kind], tok_recv.at[kind], t, h).wait_recv()

    order = (12, 14, 10, 13, 15, 11, 4, 6, 2, 5, 7, 3, 8, 9, 1)
    for n in order:
        token_copy(0, n)

    copies[0].wait()
    eye = lax.broadcasted_iota(jnp.int32, (128, 128), 0) == lax.broadcasted_iota(jnp.int32, (128, 128), 1)
    by_head = rate_all[...].astype(F32)
    for head_no in range(2 * NH):
        rate_rows[head_no, :, :ROWS] = by_head[head_no : head_no + 1]
        rate_rows[head_no, :, ROWS:] = jnp.zeros((1, 128 - ROWS), F32)
    for n in order:
        token_copy(3, n)
    for n in order:
        token_copy(1, n)

    copies[1].wait()
    copies[2].wait()
    lane = lax.broadcasted_iota(jnp.int32, (TILE, 128), 1).astype(F32)

    def look(part, slots):
        for group, slot in enumerate(slots):
            row = ids_in[slot, group : group + 1, :]
            column = jnp.sum(jnp.where(eye, row.astype(F32), 0.0), axis=1, keepdims=True)
            idcol[pl.ds(group * 128, 128), :] = jnp.broadcast_to(column, (128, 128))

        def rows_of(i, _):
            ids = idcol[span(i, TILE), :]

            def some(j, total):
                first = (j * ITEM_TILE).astype(F32)
                hot = jnp.concatenate(
                    [jnp.where(ids - first == lane + 128.0 * b, 1.0, 0.0).astype(BF16) for b in range(ITEM_TILE // 128)],
                    axis=1,
                )
                return total + dot(hot, table[span(j, ITEM_TILE), :])

            found = lax.fori_loop(0, ITEMS // ITEM_TILE, some, jnp.zeros((TILE, HD), F32))
            looked[span(2 * part + i, TILE), :] = found.astype(BF16)
            return 0

        lax.fori_loop(0, 2, rows_of, 0)

    look(0, (0, 0, 0, 0))
    for slot in (1, 2):
        remote(ids_in.at[slot], ids_in.at[slot], id_send, id_recv.at[slot - 1], t, h).wait_recv()
    look(1, (1, 1, 2, 2))

    token_wait(3)
    for s in range(SRC):
        row = jnp.where(h == s, rate_rows[2 * h + p], rb_in[s])
        column = jnp.sum(jnp.where(eye[:ROWS], row, 0.0), axis=1, keepdims=True)
        rates[pl.ds(s * ROWS, ROWS), :] = jnp.broadcast_to(column, (ROWS, 128))

    split_at = bound_ref[0]
    counts = [split_at.astype(F32), (TOKENS - split_at).astype(F32)]
    block = TOKENS // (NY * NZ)
    starts = (t * block, t * block + TILE, next_z * block, last_z * block + TILE)

    def member(segment, start, width):
        positions = start + lax.broadcasted_iota(jnp.int32, (TILE, width), 0)
        return positions < split_at if segment == 0 else positions >= split_at

    def start_of(i):
        start = starts[3]
        for j in (2, 1, 0):
            start = jnp.where(i == j, starts[j], start)
        return start

    def weighted_sum(c):
        parts = [jnp.where(member(c, starts[j], 128), rates[pl.ds(j * TILE, TILE), :], 0.0) for j in range(4)]
        return jnp.sum(parts[0] + parts[1] + parts[2] + parts[3], axis=0, keepdims=True)

    sums = [weighted_sum(c) for c in range(2)]
    rsum[...] = jnp.concatenate([jnp.broadcast_to(v, (8, 128)) for v in sums], axis=0)
    for n in range(1, NY):
        i, tok = y_peer(n)
        remote(rsum, rsum_y.at[y], rsum_send.at[0], rsum_recv.at[0], tok, h).start()
    for copy in copies[3:]:
        copy.wait()
    pltpu.make_async_copy(w, w, local_sem.at[6]).wait()

    def low(m):
        wl[m] = w[m].astype(BF16)

    for m in range(3):
        low(m)

    def queries(segment, i):
        rows = span(i, TILE)
        x = qb[rows, :]
        first_pre, third_pre = dot(x, wl[0]), dot(x, wl[1])
        act = (first_pre * sigmoid(first_pre) * third_pre).astype(BF16)
        applied = dot_cols(act, wl[2])
        if segment == 0:
            result[rows, :] = applied
        else:
            keep = member(1, start_of(i), HD)
            outb[rows, :] = jnp.where(keep, applied, result[rows, :]).astype(BF16)

    def forward(i, f):
        rows, cols = span(i, TILE), pl.ds(f * FT, FT)
        key = kb[rows, :]
        first_pre, third_pre = dot(key, wl[0, :, cols]), dot(key, wl[1, :, cols])
        s = sigmoid(first_pre)
        silu = first_pre * s
        gate[rows, cols] = silu
        slope[rows, cols] = third_pre * (s * (1.0 + first_pre * (1.0 - s)))
        acts[rows, cols] = (silu * third_pre).astype(BF16)

    def outward(c, i, f):
        rows = span(i, TILE)
        if f == 0:
            keep = member(c, starts[i], 128)
            weighted = jnp.where(keep, rates[rows, :], 0.0)
            weighted = jnp.concatenate([weighted, weighted], axis=1)
            target = vb[rows, :].astype(F32) + looked[rows, :].astype(F32)
            up[rows, :] = (-weighted * target).astype(BF16)
        part = dot_rows(up[rows, :], acts[rows, pl.ds(f * FT, FT)])
        g[2, f] = part if i == 0 else part + g[2, f]

    def backward(i, first):
        rows = span(i, TILE)
        key = kb[rows, :]
        back = dot(up[rows, :], wl[2])
        add(0, dot_rows(key, (back * slope[rows, :]).astype(BF16)), first)
        add(1, dot_rows(key, (back * gate[rows, :]).astype(BF16)), first)

    def add(m, part, first):
        for f in range(2):
            half = part[:, f * FT : (f + 1) * FT]
            if isinstance(first, bool):
                g[m, f] = half if first else half + g[m, f]
            else:
                g[m, f] = half + jnp.where(first, 0.0, g[m, f])

    chunks = ((2, 0), (2, 1), (0, 0), (0, 1), (1, 0), (1, 1))
    stages = (((y, y_peer), (zq, z_peer)), ((zq, z_peer), (y, y_peer)))

    def stages_of(k):
        return stages[1 if k == 5 else 0]

    def part_wait(k, stage, b):
        remote(b, b, part_send.at[stage], part_recv.at[k, stage], t, h).wait_recv()

    def send_first(c, k):
        (m, f), (here, peer) = chunks[k], stages_of(k)[0]
        gl[c, m, f] = g[m, f].astype(BF16)
        for n in range(1, NY):
            i, tok = peer(n)
            remote(gl.at[c, m, f, span(i, YR)], ybuf.at[c, k, here], part_send.at[0], part_recv.at[k, 0], tok, h).start()

    def reduce_first(c, k):
        (m, f), ((first, peer1), (second, peer2)) = chunks[k], stages_of(k)
        total = g[m, f, span(first, YR), :]
        part_wait(k, 0, ybuf.at[c, k, pl.ds(0, NY - 1)])
        for n in range(1, NY):
            total = total + ybuf[c, k, peer1(n)[0]].astype(F32)
        zown[k] = total
        zsend[c, k] = total.astype(BF16)
        for n in range(1, NQ):
            i, tok = peer2(n)
            remote(zsend.at[c, k, span(i, ZR)], zbuf.at[c, k, second], part_send.at[1], part_recv.at[k, 1], tok, h).start()

    def reduce_second(c, k):
        (m, f), ((first, _), (second, peer2)) = chunks[k], stages_of(k)
        total = zown[k, span(second, ZR), :]
        part_wait(k, 1, zbuf.at[c, k, pl.ds(0, NQ - 1)])
        for n in range(1, NQ):
            total = total + zbuf[c, k, peer2(n)[0]].astype(F32)
        mine = span(first * NQ + second, ZR)
        final[c, m, f, mine, :] = total.astype(BF16)
        for n in range(1, NQ):
            i, tok = peer2(n)
            b = final.at[c, m, f, mine]
            remote(b, b, part_send.at[2], part_recv.at[k, 2], tok, h).start()

    def gather_second(c, k):
        (m, f), (first, peer1) = chunks[k], stages_of(k)[0]
        part_wait(k, 2, final.at[c, m, f, pl.ds(0, (NQ - 1) * ZR)])
        for n in range(1, NY):
            i, tok = peer1(n)
            b = final.at[c, m, f, span(first, YR)]
            remote(b, b, part_send.at[3], part_recv.at[k, 3], tok, h).start()

    def gather_first(c, k):
        m, f = chunks[k]
        part_wait(k, 3, final.at[c, m, f, pl.ds(0, (NY - 1) * YR)])

    current = {}
    eye_hd = lax.broadcasted_iota(jnp.int32, (HD, HD), 0) == lax.broadcasted_iota(jnp.int32, (HD, HD), 1)

    def iterate(c, m, number):
        if number == 0:
            x = jnp.concatenate([final[c, m, 0], final[c, m, 1]], axis=1)
        else:
            x = current[m]
        xl = x.astype(BF16)
        gram = dot_cols(xl, xl)
        if number == 0:
            scale = 1.0 / (jnp.sqrt(jnp.sum(jnp.where(eye_hd, gram, 0.0), keepdims=True)) + 1e-06)
            gram = gram * (scale * scale)
        gram_low = gram.astype(BF16)
        poly = C2 * gram + C3 * dot(gram_low, gram_low)
        x = C1 * x.astype(F32) + dot(poly.astype(BF16), xl)
        current[m] = x * scale if number == 0 else x
        if number == NS_ITERS - 1:
            w[m] = w[m] - steps[c] * current[m]
            low(m)

    def rates_z():
        sums_y = rsum[...]
        b = rsum_y.at[pl.ds(0, NY - 1)]
        remote(b, b, rsum_send.at[0], rsum_recv.at[0], t, h).wait()
        for n in range(1, NY):
            sums_y = sums_y + rsum_y[y_peer(n)[0]]
        rsum_z[zq] = sums_y
        for n in range(1, NQ):
            i, tok = z_peer(n)
            remote(rsum_z.at[zq], rsum_z.at[zq], rsum_send.at[1], rsum_recv.at[1], tok, h).start()

    plan = (
        "q", "q", "q", "y0", "y1", "q", "y2", "y3", "z0", "y5",
        "y4", "z1", "z2", "z5", "z3", "a0", "z4", "a1", "a2", "a5",
        "a3", "g0", "a4", "g1", "n20", "n21", "n22", "g2", "g3", "n00",
        "n01", "g5", "g4", "n02", "n10", "n11", "n12",
    )

    for c in range(2):
        if c == 0:
            token_wait(0)
            for f in range(2):
                for i in range(LOCAL // TILE):
                    forward(i, f)
            token_wait(1)
        for f in range(2):
            for i in range(LOCAL // TILE):
                if c == 1:
                    forward(i, f)
            for i in range(LOCAL // TILE):
                outward(c, i, f)
            send_first(c, f)

        def backward_of(i, _):
            backward(i, i == 0)
            return 0

        lax.fori_loop(0, LOCAL // TILE, backward_of, 0, unroll=True)
        for k in (5, 2, 3, 4):
            send_first(c, k)
        if c == 0:
            rates_z()
        asked = 0
        for word in plan:
            kind, index = word[0], int(word[1:2] or 0)
            if kind == "q":
                if c == 1:
                    queries(0, asked)
                    asked += 1
                continue
            if c == 0 and word == "g0":
                for n in order:
                    token_copy(2, n)
            if kind == "n":
                if c == 0 and word == "n20":
                    b = rsum_z.at[pl.ds(0, NQ - 1)]
                    remote(b, b, rsum_send.at[1], rsum_recv.at[1], t, h).wait()
                    sums_all = rsum_z[0] + rsum_z[1] + rsum_z[2] + rsum_z[3]
                    steps = [sums_all[8 * i : 8 * i + 1, 0:1] / counts[i] for i in range(2)]
                iterate(c, index, int(word[2]))
            elif kind == "p":
                for number in range(NS_ITERS):
                    for m in range(2):
                        iterate(c, m, number)
            else:
                {"y": reduce_first, "z": reduce_second, "a": gather_second, "g": gather_first}[kind](c, index)
        if c == 0:
            token_wait(2)

    for k in (3, 2, 1, 0):
        queries(1, k if k > 1 else 1 - bits[2] if k else bits[2])
        for j in range(4):
            if k > 1:
                tok, head, slot = (last_z, j + 4, NH + 4 + j) if k == 3 else (next_z, j, NH + j)
            elif k or j:
                tok, head, slot = origin(4 * k + j)
            else:
                continue
            remote(outb.at[span(slot, ROWS)], out_ref.at[:, my_cols], out_send, out_recv, tok, head).start()
    mine_copy = pltpu.make_async_copy(outb.at[own], out_ref.at[:, my_cols], local_sem.at[7])
    mine_copy.start()
    for kind in range(4):
        b = all_but_one(kind)
        remote(b, b, tok_send.at[kind], tok_recv.at[kind], t, h).wait_send()
    remote(ids_in.at[pl.ds(0, 2)], ids_in.at[pl.ds(0, 2)], id_send, id_recv.at[0], t, h).wait_send()
    for stage in range(4):
        b = zsend.at[:, :, pl.ds(0, (NQ - 1) * ZR)] if stage in (1, 2) else gl.at[:, :, :, pl.ds(0, (NY - 1) * YR)]
        remote(b, b, part_send.at[stage], part_recv.at[0, stage], t, h).wait_send()
    b = out_ref.at[:, pl.ds(0, D - HD)]
    remote(b, b, out_send, out_recv, t, h).wait()
    mine_copy.wait()


def shards(queries, keys, values, rates, item_ids, boundary, item_table, w_first, w_third, w_out):
    ids = item_ids.reshape(4, 128)
    pin = lambda x: pltpu.with_memory_space_constraint(x, pltpu.HBM)
    hbm = pl.BlockSpec(memory_space=pltpu.HBM)
    dma = pltpu.SemaphoreType.DMA
    return pl.pallas_call(
        kernel,
        out_shape=jax.ShapeDtypeStruct((ROWS, D), BF16),
        in_specs=[hbm, hbm, hbm, hbm, hbm, pl.BlockSpec(memory_space=pltpu.SMEM), hbm, hbm, hbm, hbm],
        out_specs=pl.BlockSpec(memory_space=pl.ANY),
        scratch_shapes=[
            pltpu.VMEM((LOCAL, HD), BF16),
            pltpu.VMEM((LOCAL, HD), BF16),
            pltpu.VMEM((LOCAL, HD), BF16),
            pltpu.VMEM((2 * NH, ROWS), BF16),
            pltpu.VMEM((2 * NH, 1, 128), F32),
            pltpu.VMEM((SRC, 1, 128), F32),
            pltpu.VMEM((3, 4, 128), jnp.int32),
            pltpu.VMEM((ITEMS, HD), BF16),
            pltpu.VMEM((3, HD, FH), F32),
            pltpu.VMEM((3, HD, FH), BF16),
            pltpu.VMEM((LOCAL, 128), F32),
            pltpu.VMEM((512, 128), F32),
            pltpu.VMEM((LOCAL, HD), BF16),
            pltpu.VMEM((LOCAL, HD), BF16),
            pltpu.VMEM((LOCAL, FH), BF16),
            pltpu.VMEM((LOCAL, FH), F32),
            pltpu.VMEM((LOCAL, FH), F32),
            pltpu.VMEM((3, 2, HD, FT), F32),
            pltpu.VMEM((2, 3, 2, HD, FT), BF16),
            pltpu.VMEM((2, 6, NY, YR, FT), BF16),
            pltpu.VMEM((6, YR, FT), F32),
            pltpu.VMEM((2, 6, YR, FT), BF16),
            pltpu.VMEM((2, 6, NQ, ZR, FT), BF16),
            pltpu.VMEM((2, 3, 2, HD, FT), BF16),
            pltpu.VMEM((16, 128), F32),
            pltpu.VMEM((NY, 16, 128), F32),
            pltpu.VMEM((NQ, 16, 128), F32),
            pltpu.VMEM((LOCAL, HD), F32),
            pltpu.VMEM((LOCAL, HD), BF16),
            dma((4,)), dma((4,)), dma, dma((2,)), dma((4,)), dma((6, 4)), dma((2,)), dma((2,)),
            dma, dma, dma((8,)),
        ],
        compiler_params=pltpu.CompilerParams(
            collective_id=0, has_side_effects=True, vmem_limit_bytes=40 * 1024 * 1024
        ),
        name="layer",
    )(*map(pin, (queries, keys, values, rates.T, ids)), boundary, *map(pin, (item_table, w_first, w_third, w_out)))


def solution(mesh):
    in_specs = (
        P(("tok", "head"), None),
        P(("tok", "head"), None),
        P(("tok", "head"), None),
        P(("tok", "head"), None),
        P("tok"),
        P(),
        P(None, "head"),
        P("head", None, None),
        P("head", None, None),
        P("head", None, None),
    )
    out_specs = P(("tok", "head"), None)
    return jax.shard_map(shards, mesh=mesh, in_specs=in_specs, out_specs=out_specs, check_vma=False)
```
